128 devices in a mesh: dp: 2 (over y_hi), ctx: 16 (over x, z), tensor: 4 (over y_lo, core).
Axes of the slice: x: 4, y: 4 (y_hi: 2, y_lo: 2; y = y_hi * 2 + y_lo), z: 4, core: 2. Of those that a mesh axis runs over, the one named last changes fastest.
Arguments:
- values: bfloat16 [2, 4096, 4096], P('dp', 'ctx', 'tensor'), may hold values from -6 to 6
- b_proj: bfloat16 [2, 4096, 128], P('dp', 'ctx'), may hold values from -0.1875 to 0.1875
- c_proj: bfloat16 [2, 4096, 128], P('dp', 'ctx'), may hold values from -0.52734375 to 0.52734375
- step_sizes: float32 [2, 64, 4096], P('dp', 'tensor', 'ctx'), may hold values from 0.5 to 2
- decay_rates: float32 [64], P('tensor'), may hold values from 0.05 to 60
- skip_gain: float32 [64], P('tensor'), may hold values from 0.5 to 1.5
- w_out: bfloat16 [4096, 4096], P(None, 'tensor'), may hold values from -0.09375 to 0.09375
- d_out: bfloat16 [2, 4096, 4096], P('dp', 'ctx'), may hold values from -6 to 6
Outputs:
- d_values: bfloat16 [2, 4096, 4096], P('dp', 'ctx', 'tensor')
- d_b: float32 [2, 4096, 128], P('dp', 'ctx')
- d_c: float32 [2, 4096, 128], P('dp', 'ctx')
- d_steps: float32 [2, 64, 4096], P('dp', 'tensor', 'ctx')
- d_rates: float32 [64], P('tensor')
- d_skip: float32 [64], P('tensor')
- d_w: float32 [4096, 4096], P(('dp', 'ctx'), 'tensor')
The draws below stay inside these ranges and needn't reach their ends.
All inputs are finite; a program needn't handle non-finite values.
Results may differ from the reference program's by a relative error of at most 0.006.
Values sent between devices are 32-bit elements; how exact they have to be, the bound alone decides.
No kernel may reach another device: no remote copies, remote signals or barrier semaphores. Data moves between devices by JAX's collectives and lax.ppermute only.
A program may use at most 128 MiB of HBM per device.

```python
import math
import jax
import jax.numpy as jnp
from jax import lax

D = 4096
HEADS = 64
HEAD_DIM = 64
STATE = 128
INNER = 4096
SEQ = 4096
BATCH = 2


def with_spikes(values, own_key, source, target, parts, factor):
    def block_of(axis_at):
        return (jnp.arange(values.shape[axis_at]) // (values.shape[axis_at] // parts)).reshape((-1,) + (1,) * (values.ndim - 1 - axis_at))

    near = jax.random.permutation(own_key, parts)[block_of(target)]
    other_side = (block_of(target) + parts // 2) % parts
    return jnp.where((block_of(source) == near) | (block_of(source) == other_side), factor * values, values)


def shard_levels(stream_key, shape, cuts, low, high):
    gain, own = 1.0, jax.random.fold_in(stream_key, 6)
    for dim, shards_of in cuts:
        draws = jnp.exp(jax.random.uniform(jax.random.fold_in(own, dim), (shards_of,), jnp.float32, low / len(cuts), high / len(cuts)))
        gain = gain * jnp.repeat(draws, shape[dim] // shards_of).reshape([-1 if axis == dim else 1 for axis in range(len(shape))])
    return gain


def centred(stream_key, dims, scale, bound, shards=(), kind=jnp.bfloat16):
    gain = shard_levels(stream_key, dims, shards, -0.22, 0.18) if shards else 1.0
    array = jax.random.normal(stream_key, dims, jnp.float32) * scale * gain
    return jnp.minimum(jnp.maximum(array, -bound), bound).astype(kind)


def heavy_noise(stream_key, extent, deviation, limit, cuts, heavy, kind=jnp.bfloat16):
    drawn = deviation * jax.random.normal(stream_key, extent, jnp.float32)
    if cuts:
        drawn = drawn * shard_levels(stream_key, extent, cuts, -0.22, 0.18)
    return jnp.clip(with_spikes(drawn, jax.random.fold_in(stream_key, 3), *heavy), -limit, limit).astype(kind)


def setup_inputs(seed: int = 0) -> dict:
    key_of = jax.random.split(jax.random.key(seed), 9)
    return {
        "values": centred(key_of[0], (BATCH, SEQ, INNER), 1.0, 6.0, ((0, 2), (1, 16), (2, 4))),
        "b_proj": centred(key_of[1], (BATCH, SEQ, STATE), (2 * SEQ ** -0.5), 0.1875, ((0, 2), (1, 16))),
        "c_proj": centred(key_of[2], (BATCH, SEQ, STATE), (STATE ** -0.5), 0.52734375, ((0, 2), (1, 16))),
        "step_sizes": jnp.clip(jnp.exp(math.log(2.0) - 1.3862944 * jax.random.uniform(key_of[3], (BATCH, HEADS, SEQ), jnp.float32) ** shard_levels(key_of[3], (BATCH, HEADS, SEQ), ((0, 2), (1, 4), (2, 16)), -0.2, 0.2)), 0.5, 2.0),
        "decay_rates": jnp.clip(jnp.exp(math.log(60.0) - 7.090077 * jax.random.uniform(key_of[4], (HEADS,), jnp.float32) ** shard_levels(key_of[4], (HEADS,), ((0, 4),), -0.2, 0.2)), 0.05, 60.0),
        "skip_gain": jnp.clip(0.5 + 1.0 * jax.random.uniform(key_of[5], (HEADS,), jnp.float32) ** shard_levels(key_of[5], (HEADS,), ((0, 4),), -0.2, 0.2), 0.5, 1.5),
        "w_out": centred(key_of[6], (D, INNER), INNER ** -0.5, 0.09375, ((1, 4),)),
        "d_out": heavy_noise(key_of[7], (BATCH, SEQ, D), 1.0, 6.0, ((0, 2), (1, 16)), (1, 2, 16, 2.0)),
    }


high = lax.Precision.HIGHEST

def run_blocks(chan_vals, b_rows, c_rows, step_rows, rates, gains, start_state, length):
    total_len = chan_vals.shape[0]
    heads_here = chan_vals.shape[1]
    head_width = chan_vals.shape[2]
    state_width = b_rows.shape[1]
    block = min(256, total_len)
    nblocks = total_len // block
    vals_blk = chan_vals.reshape(nblocks, block, heads_here, head_width)
    b_blk = b_rows.reshape(nblocks, block, state_width)
    c_blk = c_rows.reshape(nblocks, block, state_width)
    step_blk = step_rows.reshape(heads_here, nblocks, block).transpose(1, 0, 2)
    position = jnp.arange(block)
    lower = position[:, None] >= position[None, :]

    def advance(state, pieces):
        vals_one, b_one, c_one, step_one = pieces
        logdecay = -step_one * rates[:, None] / length
        running = jnp.cumsum(logdecay, axis=1)
        between = running[:, :, None] - running[:, None, :]
        weights = jnp.exp(jnp.where(lower[None], between, -jnp.inf))
        intersection = jnp.einsum('in,jn->ij', c_one, b_one, precision=high)
        mixing = weights * intersection[None] * step_one[:, None, :]
        inside = jnp.einsum('hij,jhp->ihp', mixing, vals_one, precision=high)
        carried = jnp.exp(running).T[:, :, None] * jnp.einsum('in,hpn->ihp', c_one, state, precision=high)
        output = inside + carried + gains[None, :, None] * vals_one
        tail = jnp.exp(running[:, -1:] - running) * step_one
        fresh = jnp.einsum('hj,jhp,jn->hpn', tail, vals_one, b_one, precision=high)
        new_state = jnp.exp(running[:, -1])[:, None, None] * state + fresh
        return (new_state, output)
    end_state, outputs = lax.scan(jax.checkpoint(advance), start_state, (vals_blk, b_blk, c_blk, step_blk))
    return (outputs.reshape(total_len, heads_here, head_width), end_state)

def reference(values, b_proj, c_proj, step_sizes, decay_rates, skip_gain, w_out, d_out):

    def forward(vals, b_all, c_all, steps_all, rates, gains):

        def single(vals_one, b_one, c_one, steps_one):
            zero_state = jnp.zeros((HEADS, HEAD_DIM, STATE), jnp.float32)
            mixed, _ = run_blocks(vals_one.reshape(SEQ, HEADS, HEAD_DIM), b_one, c_one, steps_one, rates, gains, zero_state, SEQ)
            return mixed.reshape(SEQ, INNER)
        return jax.vmap(single)(vals, b_all, c_all, steps_all)
    mixed, pullback = jax.vjp(forward, values.astype(jnp.float32), b_proj.astype(jnp.float32), c_proj.astype(jnp.float32), step_sizes, decay_rates, skip_gain)
    mixed_bf = mixed.astype(jnp.bfloat16)
    upstream = jnp.stack([jnp.dot(d_out[index], w_out, preferred_element_type=jnp.float32) for index in range(BATCH)]).astype(jnp.bfloat16)
    d_w = jnp.zeros((D, INNER), jnp.float32)
    for index in range(BATCH):
        d_w = d_w + jnp.dot(d_out[index].T, mixed_bf[index], preferred_element_type=jnp.float32)
    grad_vals, grad_b, grad_c, grad_steps, grad_rates, grad_skip = pullback(upstream.astype(jnp.float32))
    return (grad_vals.astype(jnp.bfloat16), grad_b, grad_c, grad_steps, grad_rates, grad_skip, d_w)
```

```python
import jax
import jax.numpy as jnp
from jax import lax
from jax.experimental import pallas as pl
from jax.experimental.pallas import tpu as pltpu
from jax.sharding import PartitionSpec as P


f32 = jnp.float32
bf16 = jnp.bfloat16
high = lax.Precision.HIGHEST
EVERY = ("dp", "ctx", "tensor")
RING = 4
HEADS = 16
WIDTH = 64
STATE = 128
TOKENS = 256


def dot(a, b, ca, cb, precision=None):
    return lax.dot_general(
        a, b, (((ca,), (cb,)), ((), ())), precision=precision, preferred_element_type=f32
    )


def device(dp, x, z, t):
    return (dp * 16 + x * RING + z) * 4 + t


def hop(value, shift, primary):
    pairs = []
    for dp in range(2):
        for x in range(RING):
            for z in range(RING):
                for t in range(4):
                    along_x = (t % 2 == 0) == primary
                    to = (
                        device(dp, (x + shift) % RING, z, t)
                        if along_x
                        else device(dp, x, (z + shift) % RING, t)
                    )
                    pairs.append((device(dp, x, z, t), to))
    return lax.ppermute(value, EVERY, pairs)


def select_half(col0, col1):
    lane = lax.broadcasted_iota(jnp.int32, (TOKENS, 128), 1)
    return jnp.where(lane < WIDTH, col0, col1)


def slab_kernel(where, *refs):
    for src, dst in zip(refs[:RING], refs[RING:]):
        dst[...] = src[...].astype(f32)


def slabs(cotangent, primary, secondary, dp, core):
    def spec(offset):
        def at(k, where):
            p = (where[0] + offset) % RING
            s = (where[1] + k // 2) % RING
            d = (where[2] + k % 2) % 2
            col = jnp.where(where[3] == 0, p * RING + s, s * RING + p)
            return (0, d * 16 + col)

        return pl.BlockSpec((TOKENS, 128), at)

    out = jax.ShapeDtypeStruct((TOKENS, 1024), f32)
    return pl.pallas_call(
        slab_kernel,
        grid_spec=pltpu.PrefetchScalarGridSpec(
            num_scalar_prefetch=1,
            grid=(8,),
            in_specs=[spec(o) for o in range(RING)],
            out_specs=[pl.BlockSpec((TOKENS, 128), lambda k, where: (0, k))] * RING,
        ),
        out_shape=[out] * RING,
        name="slabs",
    )(jnp.stack([primary, secondary, dp, core]).astype(jnp.int32), *[cotangent] * RING)


def ends_kernel(v_ref, u_ref, b_ref, c_ref, col_ref, row_ref, out_ref):
    col = col_ref[0]
    tail = select_half(col[:, 2:3], col[:, 3:4])
    grow = select_half(col[:, 4:5], col[:, 5:6])
    left = (v_ref[...].astype(f32) * tail).astype(bf16)
    right = (u_ref[...].astype(f32) * grow).astype(bf16)
    end = dot(left, b_ref[...], 0, 0)
    grad = dot(right, c_ref[...], 0, 0)
    for h in range(2):
        out_ref[h, 0:64, :] = end[h * 64 : h * 64 + 64]
        out_ref[h, 64:128, :] = grad[h * 64 : h * 64 + 64]
        out_ref[h, 128:136, :] = jnp.broadcast_to(row_ref[0, 4 + h : 5 + h, 0:128], (8, 128))


def chain_kernel(in_ref, out_ref):
    count = in_ref.shape[0]
    state = jnp.zeros((64, 128), f32)
    for i in range(count):
        out_ref[i, 0:64, :] = state
        state = in_ref[i, 128:129, :] * state + in_ref[i, 0:64, :]
    state = jnp.zeros((64, 128), f32)
    for i in reversed(range(count)):
        out_ref[i, 64:128, :] = state
        state = in_ref[i, 128:129, :] * state + in_ref[i, 64:128, :]


def mix_kernel(
    v_ref, u_ref, b_ref, c_ref, col_ref, row_ref, st_ref, gain_ref,
    top_ref, bot_ref, dv_ref, rows_ref, dbc_ref, cb_ref, dq_ref,
):
    step = pl.program_id(0)
    b = b_ref[...]
    c = c_ref[...]

    @pl.when(step == 0)
    def _():
        cb_ref[...] = dot(c, b, 1, 1)
        dq_ref[...] = jnp.zeros_like(dq_ref)
        dbc_ref[...] = jnp.zeros_like(dbc_ref)

    col = col_ref[0]
    rows = row_ref[0]
    v = v_ref[...]
    u = u_ref[...]
    vf = v.astype(f32)
    uf = u.astype(f32)
    tail = select_half(col[:, 2:3], col[:, 3:4])
    grow = select_half(col[:, 4:5], col[:, 5:6])
    lane = lax.broadcasted_iota(jnp.int32, (TOKENS, 128), 1)
    at_row = lax.broadcasted_iota(jnp.int32, (TOKENS, TOKENS), 0)
    at_col = lax.broadcasted_iota(jnp.int32, (TOKENS, TOKENS), 1)
    lower = at_row >= at_col
    inside = []
    back = []
    for h in range(2):
        mine = (lane < WIDTH) if h == 0 else (lane >= WIDTH)
        between = jnp.where(lower, col[:, h : h + 1] - rows[h : h + 1, :], -1e30)
        weights = jnp.exp(between) * rows[2 + h : 3 + h, :]
        mixing = (weights * cb_ref[...]).astype(bf16)
        uh = jnp.where(mine, uf, 0.0).astype(bf16)
        dq_ref[...] += dot(uh, v, 1, 1) * weights
        inside.append(dot(mixing, v, 1, 0))
        back.append(dot(mixing, u, 0, 0))
    state = jnp.concatenate([st_ref[0, 0:64, :], st_ref[1, 0:64, :]], axis=0)
    grad = jnp.concatenate([st_ref[0, 64:128, :], st_ref[1, 64:128, :]], axis=0)
    state_bf = state.astype(bf16)
    grad_bf = grad.astype(bf16)
    out = jnp.where(lane < WIDTH, inside[0], inside[1]) + grow * dot(c, state_bf, 1, 1)
    late = tail * dot(b, grad_bf, 1, 1)
    dv = jnp.where(lane < WIDTH, back[0], back[1]) + late
    gain = gain_ref[...]
    mixed = out + gain * vf
    top_ref[...] = mixed[0:128].astype(bf16).astype(f32)
    bot_ref[...] = mixed[128:256].astype(bf16).astype(f32)
    dv_ref[...] = (dv + gain * uf).astype(bf16)
    dbc_ref[0] += dot((vf * tail).astype(bf16), grad_bf, 1, 0)
    dbc_ref[1] += dot((uf * grow).astype(bf16), state_bf, 1, 0)
    pick_row = lax.broadcasted_iota(jnp.int32, (8, 128), 0)
    pick_lane = lax.broadcasted_iota(jnp.int32, (8, 128), 1)
    sums = jnp.zeros((8, TOKENS), f32)
    for k, part in enumerate((uf * out, vf * dv, vf * late, uf * vf)):
        pick = jnp.where(pick_row == 2 * k + (pick_lane >= WIDTH).astype(jnp.int32), 1.0, 0.0)
        sums = sums + dot(pick, part, 1, 1, high)
    rows_ref[0, 0:8, :] = sums
    both = state * grad
    rows_ref[0, 8:16, :] = jnp.zeros((8, TOKENS), f32)
    rows_ref[0, 8:9, 0:128] = jnp.sum(both[0:64], axis=0, keepdims=True)
    rows_ref[0, 9:10, 0:128] = jnp.sum(both[64:128], axis=0, keepdims=True)

    @pl.when(step == pl.num_programs(0) - 1)
    def _():
        dq = dq_ref[...].astype(bf16)
        dbc_ref[0] += dot(dq, c, 0, 0)
        dbc_ref[1] += dot(dq, b, 1, 0)


def weight_kernel(*refs):
    pairs = refs[:-2]
    total = None
    half = len(pairs) // 2
    for left, right in zip(pairs[:half], pairs[half:]):
        term = dot(left[...].astype(bf16), right[...].astype(bf16), 0, 0)
        total = term if total is None else total + term
    refs[-2][...] = total[0:128]
    refs[-1][...] = total[128:256]


def weight_piece(lefts, tops, bots, k):
    args = []
    specs = []
    for left in lefts:
        for half in range(2):
            args.append(left)
            specs.append(pl.BlockSpec((128, 256), lambda i, half=half: (half, k)))
    for top, bot in zip(tops, bots):
        for part in (top, bot):
            args.append(part)
            specs.append(pl.BlockSpec((128, 512), lambda i: (0, i)))
    out = jax.ShapeDtypeStruct((128, 1024), f32)
    return pl.pallas_call(
        weight_kernel,
        grid=(2,),
        in_specs=specs,
        out_specs=[pl.BlockSpec((128, 512), lambda i: (0, i))] * 2,
        out_shape=[out, out],
        name="weight_piece",
    )(*args)


def body(values, b_proj, c_proj, step_sizes, decay_rates, skip_gain, w_out, d_out):
    length = TOKENS * lax.axis_size("ctx")
    dp = lax.axis_index("dp")
    ctx = lax.axis_index("ctx")
    core = lax.axis_index("tensor") % 2
    x, z = ctx // RING, ctx % RING
    primary = jnp.where(core == 0, x, z)
    secondary = jnp.where(core == 0, z, x)
    v, b, c, dt, cotangent = values[0], b_proj[0], c_proj[0], step_sizes[0], d_out[0]

    own, for_next, for_far, for_prev = slabs(cotangent, primary, secondary, dp, core)
    left_prev = hop(for_next, 1, True)
    left_next = hop(for_prev, -1, True)
    left_far = hop(for_far, 2, True)

    upstream = jnp.dot(cotangent, w_out, preferred_element_type=f32).astype(bf16)
    position = jnp.arange(TOKENS)
    upper = (position[:, None] <= position[None, :]).astype(f32)
    running = jnp.dot(-dt * decay_rates[:, None] / length, upper, precision=high)
    total = running[:, -1:]
    tail = jnp.exp(total - running) * dt
    grow = jnp.exp(running)
    ends = jnp.broadcast_to(jnp.exp(total), running.shape)
    pack = lambda *parts: jnp.concatenate(
        [part.reshape(8, 2, TOKENS) for part in parts], axis=1
    )
    cols = pack(running, tail, grow, ends).transpose(0, 2, 1)
    rows = pack(running, dt, ends, ends)

    pair = pl.BlockSpec((TOKENS, 128), lambda g: (0, g))
    whole = pl.BlockSpec((TOKENS, STATE), lambda g: (0, 0))
    col_spec = pl.BlockSpec((1, TOKENS, 8), lambda g: (g, 0, 0))
    row_spec = pl.BlockSpec((1, 8, TOKENS), lambda g: (g, 0, 0))
    local = pl.pallas_call(
        ends_kernel,
        grid=(8,),
        in_specs=[pair, pair, whole, whole, col_spec, row_spec],
        out_specs=pl.BlockSpec((2, 136, 128), lambda g: (g, 0, 0)),
        out_shape=jax.ShapeDtypeStruct((HEADS, 136, 128), f32),
        name="ends",
    )(v, upstream, b, c, cols, rows)
    swapped = lax.all_to_all(local, "ctx", 0, 0, tiled=True)
    chained = pl.pallas_call(
        chain_kernel,
        out_shape=jax.ShapeDtypeStruct((HEADS, 128, 128), f32),
        name="chain",
    )(swapped)
    states = lax.all_to_all(chained, "ctx", 0, 0, tiled=True)

    gains = jnp.repeat(skip_gain, WIDTH).reshape(1, HEADS * WIDTH)
    half = pl.BlockSpec((128, 128), lambda g: (0, g))
    top, bot, d_values, sums, dbc = pl.pallas_call(
        mix_kernel,
        grid=(8,),
        in_specs=[
            pair, pair, whole, whole, col_spec, row_spec,
            pl.BlockSpec((2, 128, 128), lambda g: (g, 0, 0)),
            pl.BlockSpec((1, 128), lambda g: (0, g)),
        ],
        out_specs=[
            half, half, pair,
            pl.BlockSpec((1, 16, TOKENS), lambda g: (g, 0, 0)),
            pl.BlockSpec((2, TOKENS, STATE), lambda g: (0, 0, 0)),
        ],
        out_shape=[
            jax.ShapeDtypeStruct((128, 1024), f32),
            jax.ShapeDtypeStruct((128, 1024), f32),
            jax.ShapeDtypeStruct((TOKENS, 1024), bf16),
            jax.ShapeDtypeStruct((8, 16, TOKENS), f32),
            jax.ShapeDtypeStruct((2, TOKENS, STATE), f32),
        ],
        scratch_shapes=[pltpu.VMEM((TOKENS, TOKENS), f32), pltpu.VMEM((TOKENS, TOKENS), f32)],
        name="mix",
    )(v, upstream, b, c, cols, rows, states, gains)

    top_prev = hop(top, 1, True)
    bot_next = hop(bot, -1, True)
    bot_prev = hop(bot, 1, True)
    top_next = hop(top, -1, True)
    top_far = hop(top_prev, 1, True)
    bot_far = hop(bot_next, -1, True)

    part = lambda k: sums[:, k : k + 2].reshape(HEADS, TOKENS)
    from_u, from_v, from_late, from_skip = part(0), part(2), part(4), part(6)
    carried = jnp.sum(from_late, axis=1, keepdims=True) + jnp.exp(total) * jnp.sum(
        part(8), axis=1, keepdims=True
    )
    d_log = jnp.dot(from_u - from_v, upper.T, precision=high) + carried
    d_steps = from_v / dt - decay_rates[:, None] / length * d_log
    small = jnp.stack(
        [jnp.sum(-dt / length * d_log, axis=1), jnp.sum(from_skip, axis=1)]
    )
    small = lax.psum(small, ("dp", "ctx"))
    dbc = dbc + lax.ppermute(dbc, "tensor", [(t, t ^ 1) for t in range(4)])
    dbc = dbc + lax.ppermute(dbc, "tensor", [(t, t ^ 2) for t in range(4)])

    lefts = (own, left_prev, left_next, left_far)
    tops = (top, top_prev, top_next, top_far)
    bots = (bot, bot_prev, bot_next, bot_far)
    far_mine, far_other = weight_piece(lefts, tops, bots, 2)
    via_next = hop(far_mine, 1, False)
    via_prev = hop(far_other, -1, False)
    next_mine, next_other = weight_piece(lefts, tops, bots, 1)
    prev_mine, prev_other = weight_piece(lefts, tops, bots, 3)
    got_other = hop(next_other, 1, False)
    got_mine = hop(prev_mine, -1, False)
    own_mine, own_other = weight_piece(lefts, tops, bots, 0)
    more_other = hop(prev_other + via_prev, -1, False)
    more_mine = hop(next_mine + via_next, 1, False)
    away = lax.ppermute(own_other + got_other + more_other, "dp", [(0, 1), (1, 0)])
    d_w = own_mine + got_mine + more_mine + away
    return (d_values[None], dbc[0][None], dbc[1][None], d_steps[None], small[0], small[1], d_w)


def solution(mesh):
    return jax.shard_map(
        body,
        mesh=mesh,
        in_specs=(
            P("dp", "ctx", "tensor"),
            P("dp", "ctx", None),
            P("dp", "ctx", None),
            P("dp", "tensor", "ctx"),
            P("tensor"),
            P("tensor"),
            P(None, "tensor"),
            P("dp", "ctx", None),
        ),
        out_specs=(
            P("dp", "ctx", "tensor"),
            P("dp", "ctx", None),
            P("dp", "ctx", None),
            P("dp", "tensor", "ctx"),
            P("tensor"),
            P("tensor"),
            P(("dp", "ctx"), "tensor"),
        ),
        check_vma=False,
    )
```
